256 devices in a mesh: seq: 64 (over x, y, z_hi, core), head: 4 (over z_lo).
Axes of the slice: x: 4, y: 4, z: 8 (z_hi: 2, z_lo: 4; z = z_hi * 4 + z_lo), core: 2. Of those that a mesh axis runs over, the one named last changes fastest.
Arguments:
- q_rows: float32 [16384, 2048], P(('seq', 'head')), may hold values from -4 to 4
- k_rows: float32 [16384, 2048], P(('seq', 'head')), may hold values from -4 to 4
- v_rows: float32 [16384, 2048], P(('seq', 'head')), may hold values from -6 to 6
- step_sizes: float32 [8, 16384], P('head', 'seq'), may hold values from 0.1 to 1
- fast_weights: float32 [3, 8, 256, 512], P(None, 'head'), may hold values from -0.375 to 0.375
- norm_gain: float32 [2048], P('head'), may hold values from 0.1 to 1.9
- w_out: bfloat16 [2048, 4096], P('head'), may hold values from -0.125 to 0.125
Outputs:
- mixed_out: bfloat16 [16384, 4096], P(('seq', 'head'))
- new_weights: float32 [3, 8, 256, 512], P(None, 'head')
The draws below stay inside these ranges and needn't reach their ends.
All inputs are finite; a program needn't handle non-finite values.
Results may differ from the reference program's by a relative error of at most 0.005.
Values sent between devices are 32-bit elements; how exact they have to be, the bound alone decides.
No kernel may reach another device: no remote copies, remote signals or barrier semaphores. Data moves between devices by JAX's collectives and lax.ppermute only.
A program may use at most 128 MiB of HBM per device.

```python
import math
import jax
import jax.numpy as jnp
from jax import lax

D = 4096
H = 8
DH = 256
HID = 512
WINDOW = 256
NS_ITERS = 3
TOKENS = 16384
HD = 2048


def drawn_pair(key):
    base_key = jax.random.fold_in(key, 7)
    subkeys = jax.random.split(base_key, 4)
    query_part = jnp.clip(jax.random.normal(subkeys[2], (TOKENS, HD), jnp.float32), -4.0, 4.0)
    key_part = jnp.clip(jax.random.normal(subkeys[3], (TOKENS, HD), jnp.float32), -4.0, 4.0)
    return (query_part, key_part)


def draw_q_rows(key, part):
    return drawn_pair(key)[0]


def draw_k_rows(key, part):
    return drawn_pair(key)[1]


def level_of(stream_key, dims, cuts, least, largest):
    factor_of, own = 1.0, jax.random.fold_in(stream_key, 6)
    for axis_at, parts in cuts:
        heights = jnp.exp(jax.random.uniform(jax.random.fold_in(own, axis_at), (parts,), jnp.float32, least / len(cuts), largest / len(cuts)))
        factor_of = factor_of * jnp.repeat(heights, dims[axis_at] // parts).reshape([-1 if axis == axis_at else 1 for axis in range(len(dims))])
    return factor_of


def bell_draw(rng, extent, scale, most, cuts=(), kind=jnp.bfloat16):
    values = jax.random.normal(rng, extent, jnp.float32) * scale
    if len(cuts) > 0:
        values = level_of(rng, extent, cuts, -0.22, 0.18) * values
    return jnp.clip(values, min=-most, max=most).astype(kind)


def setup_inputs(seed: int = 0) -> dict:
    key_list = jax.random.split(jax.random.key(seed), 8)
    q_rows = draw_q_rows(jax.random.fold_in(key_list[7], 71), 0)
    k_rows = draw_k_rows(jax.random.fold_in(key_list[7], 71), 0)
    v_rows = bell_draw(key_list[2], (TOKENS, HD), 1.0, 6.0, ((0, 256),), jnp.float32)
    step_sizes = jnp.clip(jnp.exp(math.log(1.0) - 2.3025851 * jax.random.uniform(key_list[3], (H, TOKENS), jnp.float32) ** level_of(key_list[3], (H, TOKENS), ((0, 4), (1, 64)), -0.2, 0.2)), 0.1, 1.0)
    fast_weights = bell_draw(key_list[4], (3, H, DH, HID), DH ** -0.5, 0.375, ((1, 4),), jnp.float32)
    norm_gain = jnp.clip(1.0 + 0.18 * jax.random.normal(key_list[5], (HD,), jnp.float32), 0.1, 1.9)
    w_out = bell_draw(key_list[6], (HD, D), HD ** -0.5, 0.125, ((0, 4),))
    return dict(q_rows=q_rows, k_rows=k_rows, v_rows=v_rows, step_sizes=step_sizes, fast_weights=fast_weights, norm_gain=norm_gain, w_out=w_out)


highest = lax.Precision.HIGHEST
epsilon = 1e-06
coef_linear = 3.4445
coef_square = -4.775
coef_cubic = 2.0315

def silu_parts(pre_act):
    sigmoid_gate = jax.nn.sigmoid(pre_act)
    return (pre_act * sigmoid_gate, sigmoid_gate)

def fast_gradients(key_heads, value_heads, step_sizes, weights):
    gate_pre = jnp.einsum('hnd,hdj->hnj', key_heads, weights[0], precision=highest)
    up_pre = jnp.einsum('hnd,hdj->hnj', key_heads, weights[2], precision=highest)
    active, sigmoid_gate = silu_parts(gate_pre)
    glu_out = active * up_pre
    upstream = -step_sizes[:, :, None] * value_heads
    grad_two = jnp.einsum('hnd,hnj->hdj', upstream, glu_out, precision=highest)
    upstream_glu = jnp.einsum('hnd,hdj->hnj', upstream, weights[1], precision=highest)
    grad_three = jnp.einsum('hnd,hnj->hdj', key_heads, upstream_glu * active, precision=highest)
    slope = sigmoid_gate * (1.0 + gate_pre * (1.0 - sigmoid_gate))
    grad_one = jnp.einsum('hnd,hnj->hdj', key_heads, upstream_glu * up_pre * slope, precision=highest)
    return jnp.stack([grad_one, grad_two, grad_three])

def orthogonalize(gradients):
    inverse_norm = 1.0 / (jnp.sqrt(lax.optimization_barrier(jnp.sum(gradients * gradients, axis=(2, 3), keepdims=True))) + epsilon)
    matrix = gradients * inverse_norm
    for iteration in range(NS_ITERS):
        gram_matrix = jnp.einsum('chdj,chej->chde', matrix, matrix, precision=highest)
        polynomial = coef_square * gram_matrix + coef_cubic * jnp.einsum('chde,chef->chdf', gram_matrix, gram_matrix, precision=highest)
        matrix = coef_linear * matrix + jnp.einsum('chde,chej->chdj', polynomial, matrix, precision=highest)
    return matrix

def renormalize(old_weights, candidate):
    target = jnp.sqrt(lax.optimization_barrier(jnp.sum(old_weights * old_weights, axis=2, keepdims=True)))
    current = jnp.sqrt(lax.optimization_barrier(jnp.sum(candidate * candidate, axis=2, keepdims=True))) + epsilon
    return candidate * (target / current)

def window_attention(queries, key_rows, value_rows):
    block_rows = math.gcd(TOKENS, 512)
    padding = jnp.zeros((WINDOW, H, DH), jnp.float32)
    padded_keys = jnp.concatenate([padding, key_rows], axis=0)
    padded_values = jnp.concatenate([padding, value_rows], axis=0)

    def one_block(first_row):
        query_block = lax.dynamic_slice_in_dim(queries, first_row, block_rows, 0)
        key_block = lax.dynamic_slice_in_dim(padded_keys, first_row, block_rows + WINDOW, 0)
        value_block = lax.dynamic_slice_in_dim(padded_values, first_row, block_rows + WINDOW, 0)
        query_pos = first_row + jnp.arange(block_rows, dtype=jnp.int32)
        key_pos = first_row - WINDOW + jnp.arange(block_rows + WINDOW, dtype=jnp.int32)
        allowed = (key_pos[None, :] <= query_pos[:, None]) & (key_pos[None, :] > query_pos[:, None] - WINDOW) & (key_pos[None, :] >= 0)
        scores = jnp.einsum('qhd,khd->hqk', query_block, key_block, precision=highest) / math.sqrt(DH)
        scores = jnp.where(allowed[None], scores, -1e+30)
        highest_score = lax.optimization_barrier(jnp.max(scores, axis=-1, keepdims=True))
        expo = jnp.exp(scores - highest_score)
        attention_weights = expo / lax.optimization_barrier(jnp.sum(expo, axis=-1, keepdims=True))
        return jnp.einsum('hqk,khd->qhd', attention_weights, value_block, precision=highest)
    starts = jnp.arange(TOKENS // block_rows, dtype=jnp.int32) * block_rows
    result = lax.map(one_block, starts)
    return result.reshape(TOKENS, H, DH)

def reference(q_rows, k_rows, v_rows, step_sizes, fast_weights, norm_gain, w_out):
    queries = q_rows.reshape(TOKENS, H, DH)
    key_rows = k_rows.reshape(TOKENS, H, DH)
    value_rows = v_rows.reshape(TOKENS, H, DH)
    gradients = fast_gradients(key_rows.transpose(1, 0, 2), value_rows.transpose(1, 0, 2), step_sizes, fast_weights)
    orthogonal = orthogonalize(gradients)
    new_weights = renormalize(fast_weights, fast_weights - orthogonal)
    query_heads = queries.transpose(1, 0, 2)
    gate_pre = jnp.einsum('hnd,hdj->hnj', query_heads, new_weights[0], precision=highest)
    up_pre = jnp.einsum('hnd,hdj->hnj', query_heads, new_weights[2], precision=highest)
    active, sigmoid_gate = silu_parts(gate_pre)
    fast_out = jnp.einsum('hnj,hdj->hnd', active * up_pre, new_weights[1], precision=highest)
    fast_out = fast_out * lax.rsqrt(lax.optimization_barrier(jnp.mean(fast_out * fast_out, axis=-1, keepdims=True)) + epsilon)
    fast_out = fast_out * norm_gain.reshape(H, 1, DH)
    attended = window_attention(queries, key_rows, value_rows)
    combined = (fast_out.transpose(1, 0, 2) + attended).reshape(TOKENS, HD).astype(jnp.bfloat16)
    mixed_out = jnp.dot(combined, w_out, preferred_element_type=jnp.float32).astype(jnp.bfloat16)
    return (mixed_out, new_weights)
```

```python
import math
import jax
import jax.numpy as jnp
from jax import lax
from jax.experimental import pallas as pl
from jax.experimental.pallas import tpu as pltpu
from jax.sharding import Mesh, PartitionSpec as P


NS_ITERS = 3
epsilon = 1e-06
coef_linear = 3.4445
coef_square = -4.775
coef_cubic = 2.0315


def split(value):
    high = value.astype(jnp.bfloat16)
    low = (value - high.astype(jnp.float32)).astype(jnp.bfloat16)
    return high, low


def dot3(left, right, contract):
    dims = (contract, ((), ()))
    (lh, ll), (rh, rl) = left, right
    prod = lambda a, b: lax.dot_general(a, b, dims, preferred_element_type=jnp.float32)
    return prod(lh, rh) + (prod(lh, rl) + prod(ll, rh))


NN = ((1,), (0,))
NT = ((1,), (1,))
TN = ((0,), (0,))


def rows_of(ref):
    return ref[...].reshape(-1, ref.shape[-1])


def joined(*refs):
    return jnp.concatenate([ref[...] for ref in refs], axis=0)


def gradient_kernel(k_ref, v_ref, s_ref, w_ref, g_ref):
    key = split(rows_of(k_ref))
    upstream = split(-s_ref[...] * rows_of(v_ref))
    gate_pre = dot3(key, split(w_ref[0]), NN)
    up_pre = dot3(key, split(w_ref[2]), NN)
    back = dot3(upstream, split(w_ref[1]), NN)
    sig = jax.nn.sigmoid(gate_pre)
    active = gate_pre * sig
    g_ref[1] = dot3(upstream, split(active * up_pre), TN)
    g_ref[2] = dot3(key, split(back * active), TN)
    slope = sig * (1.0 + gate_pre * (1.0 - sig))
    g_ref[0] = dot3(key, split(back * up_pre * slope), TN)


def newton_kernel(g_ref, w_ref, o_ref):
    mats = []
    for i in range(3):
        g = g_ref[i]
        mats.append(g * (1.0 / (jnp.sqrt(jnp.sum(g * g, keepdims=True)) + epsilon)))
    for _ in range(NS_ITERS):
        parts = [split(m) for m in mats]
        grams = [dot3(p, p, NT) for p in parts]
        gparts = [split(a) for a in grams]
        polys = [coef_square * a + coef_cubic * dot3(p, p, NN) for a, p in zip(grams, gparts)]
        mats = [coef_linear * m + dot3(split(b), p, NN) for m, b, p in zip(mats, polys, parts)]
    for i in range(3):
        w = w_ref[i]
        c = w - mats[i]
        target = jnp.sqrt(jnp.sum(w * w, axis=0, keepdims=True))
        current = jnp.sqrt(jnp.sum(c * c, axis=0, keepdims=True)) + epsilon
        o_ref[i] = c * (target / current)


def attention_kernel(first_ref, order_ref, qa, qb, qc, qd, kp_ref, k_ref, vp_ref, v_ref, o_ref):
    q = split(joined(qa, qb, qc, qd))
    scale = 1.0 / math.sqrt(o_ref.shape[-1])
    prev = dot3(q, split(rows_of(kp_ref)), NT) * scale
    here = dot3(q, split(rows_of(k_ref)), NT) * scale
    row = lax.broadcasted_iota(jnp.int32, prev.shape, 0)
    col = lax.broadcasted_iota(jnp.int32, prev.shape, 1)
    prev = jnp.where((col > row) & (first_ref[0] > 0), prev, -1e30)
    here = jnp.where(col <= row, here, -1e30)
    top = jnp.maximum(jnp.max(prev, axis=1, keepdims=True), jnp.max(here, axis=1, keepdims=True))
    ep, eh = jnp.exp(prev - top), jnp.exp(here - top)
    total = jnp.sum(ep, axis=1, keepdims=True) + jnp.sum(eh, axis=1, keepdims=True)
    acc = dot3(split(ep), split(rows_of(vp_ref)), NN) + dot3(split(eh), split(rows_of(v_ref)), NN)
    o_ref[...] = acc / total


def apply_head(qa, qb, qc, qd, w_ref, att_ref, gain_ref):
    q = split(joined(qa, qb, qc, qd))
    gate_pre = dot3(q, split(w_ref[0]), NN)
    up_pre = dot3(q, split(w_ref[2]), NN)
    glu = gate_pre * jax.nn.sigmoid(gate_pre) * up_pre
    fast = dot3(split(glu), split(w_ref[1]), NT)
    fast = fast * lax.rsqrt(jnp.mean(fast * fast, axis=1, keepdims=True) + epsilon)
    return fast * gain_ref[...] + att_ref[...]


def apply_first_kernel(head_ref, order_ref, *refs):
    *given, o_ref = refs
    o_ref[...] = apply_head(*given)


def apply_second_kernel(head_ref, order_ref, *refs):
    *given, done_ref, o_ref = refs
    value = apply_head(*given)
    done = done_ref[...]
    is_first = head_ref[0] == 0
    dim = value.shape[1]
    o_ref[:, :dim] = jnp.where(is_first, value, done).astype(o_ref.dtype)
    o_ref[:, dim:] = jnp.where(is_first, done, value).astype(o_ref.dtype)


SEQ = ("x", "y", "zh", "core")
HEAD_DIM = 256


def head_gradient(pairs, steps, weights, head):
    dim, hidden = weights.shape[2:]
    length = steps.shape[1]
    ranks, _, rows, _ = pairs.shape
    spec = pltpu.PrefetchScalarGridSpec(
        num_scalar_prefetch=1,
        grid=(1,),
        in_specs=[
            pl.BlockSpec((ranks, None, rows, dim), lambda i, h: (0, 0, 0, h[0])),
            pl.BlockSpec((ranks, None, rows, dim), lambda i, h: (0, 1, 0, h[0])),
            pl.BlockSpec((None, length, 1), lambda i, h: (h[0], 0, 0)),
            pl.BlockSpec((3, None, dim, hidden), lambda i, h: (0, h[0], 0, 0)),
        ],
        out_specs=pl.BlockSpec((3, dim, hidden), lambda i, h: (0, 0, 0)),
    )
    return pl.pallas_call(
        lambda h, *refs: gradient_kernel(*refs),
        grid_spec=spec,
        out_shape=jax.ShapeDtypeStruct((3, dim, hidden), jnp.float32),
        name="gradient",
    )(head, pairs, pairs, steps, weights)


def newton(grads, weights, head):
    _, dim, hidden = grads.shape
    spec = pltpu.PrefetchScalarGridSpec(
        num_scalar_prefetch=1,
        grid=(1,),
        in_specs=[
            pl.BlockSpec((3, dim, hidden), lambda i, h: (0, 0, 0)),
            pl.BlockSpec((3, None, dim, hidden), lambda i, h: (0, h[0], 0, 0)),
        ],
        out_specs=pl.BlockSpec((3, dim, hidden), lambda i, h: (0, 0, 0)),
    )
    return pl.pallas_call(
        lambda h, *refs: newton_kernel(*refs),
        grid_spec=spec,
        out_shape=jax.ShapeDtypeStruct((3, dim, hidden), jnp.float32),
        name="newton",
    )(head, grads, weights)


def query_specs(rows, dim, column):
    def block(source):
        return pl.BlockSpec(
            (None, rows, dim), lambda i, f, order: (order[source], 0, column(i, f))
        )

    return [block(source) for source in range(4)]


def attention(first, order, queries, before, pairs):
    ranks, _, rows, width = pairs.shape
    dim = HEAD_DIM
    length = ranks * rows
    key = pl.BlockSpec((ranks, None, rows, dim), lambda i, f, order: (0, 0, 0, i))
    value = pl.BlockSpec((ranks, None, rows, dim), lambda i, f, order: (0, 1, 0, i))
    return pl.pallas_call(
        attention_kernel,
        grid_spec=pltpu.PrefetchScalarGridSpec(
            num_scalar_prefetch=2,
            grid=(width // dim,),
            in_specs=[*query_specs(rows, dim, lambda i, f: i), key, key, value, value],
            out_specs=pl.BlockSpec((length, dim), lambda i, f, order: (0, i)),
        ),
        out_shape=jax.ShapeDtypeStruct((length, width), jnp.float32),
        name="attention",
    )(first, order, *[queries] * 4, before, pairs, before, pairs)


def apply_fast(head, order, queries, weights, attended, gain, done=None):
    ranks, rows, width = queries.shape
    length = ranks * rows
    _, dim, hidden = weights.shape
    specs = [
        *query_specs(rows, dim, lambda i, h: h[0]),
        pl.BlockSpec((3, dim, hidden), lambda i, h, order: (0, 0, 0)),
        pl.BlockSpec((length, dim), lambda i, h, order: (0, h[0])),
        pl.BlockSpec((1, dim), lambda i, h, order: (0, h[0])),
    ]
    if done is not None:
        specs.append(pl.BlockSpec((length, dim), lambda i, h, order: (0, 0)))
    extent = dim if done is None else width
    return pl.pallas_call(
        apply_first_kernel if done is None else apply_second_kernel,
        grid_spec=pltpu.PrefetchScalarGridSpec(
            num_scalar_prefetch=2,
            grid=(1,),
            in_specs=specs,
            out_specs=pl.BlockSpec((length, extent), lambda i, h, order: (0, 0)),
        ),
        out_shape=jax.ShapeDtypeStruct(
            (length, extent), jnp.float32 if done is None else jnp.bfloat16
        ),
        name="apply_first" if done is None else "apply_second",
    )(head, order, *[queries] * 4, weights, attended, gain, *(() if done is None else (done,)))


def by_head(rows):
    length, width = rows.shape
    return rows.reshape(length, 4, width // 4).transpose(1, 0, 2)


def exchange(value, axes):
    return lax.all_to_all(value, axes, split_axis=0, concat_axis=0, tiled=True)


def rotated_heads(rows):
    width = rows.shape[1] // 4
    here = lax.axis_index("head")
    parts = []
    for step in range(4):
        column = lax.rem(here + step, 4) * width
        part = lax.dynamic_slice_in_dim(rows, column, width, axis=1)
        if step:
            part = lax.ppermute(part, "head", [(rank, (rank + step) % 4) for rank in range(4)])
        parts.append(part)
    order = jnp.stack([lax.rem(here + 4 - source, 4) for source in range(4)])
    return jnp.stack(parts), order


def swap_cores(value):
    return lax.ppermute(value, "core", [(0, 1), (1, 0)])


def sum_rest(value):
    shape = value.shape
    pieces = exchange(value.reshape(16, -1, shape[-1]), ("x", "y"))
    part = jnp.sum(pieces, axis=0)
    part = part + lax.ppermute(part, "zh", [(0, 1), (1, 0)])
    return exchange(jnp.broadcast_to(part, (16, *part.shape)), ("x", "y")).reshape(shape)


def earlier(value):
    return lax.ppermute(value, SEQ, [(source, source + 1) for source in range(63)])


def local(q_rows, k_rows, v_rows, step_sizes, fast_weights, norm_gain, w_out):
    core = lax.axis_index("core")
    mine, other = core.reshape(1), (1 - core).reshape(1)
    first = lax.axis_index(SEQ).reshape(1)
    steps = step_sizes[:, :, None]
    gain = norm_gain.reshape(1, -1)
    pairs = exchange(jnp.stack([by_head(k_rows), by_head(v_rows)], axis=1), "head")
    given = head_gradient(pairs, steps, fast_weights, other)
    received = swap_cores(given)
    kept = head_gradient(pairs, steps, fast_weights, mine)
    before = earlier(pairs)
    total = sum_rest(kept + received)
    updated = newton(total, fast_weights, mine)
    partner = swap_cores(updated)
    queries, order = rotated_heads(q_rows)
    attended = attention(first, order, queries, before, pairs)
    done = apply_fast(mine, order, queries, updated, attended, gain)
    combined = apply_fast(other, order, queries, partner, attended, gain, done)
    partial = jnp.dot(combined, w_out, preferred_element_type=jnp.float32)
    mixed = lax.psum_scatter(partial, "head", scatter_dimension=0, tiled=True)
    own, swapped = updated[:, None], partner[:, None]
    new_weights = jnp.where(
        core == 0,
        jnp.concatenate([own, swapped], axis=1),
        jnp.concatenate([swapped, own], axis=1),
    )
    return (mixed.astype(jnp.bfloat16), new_weights)


def solution(mesh):
    mesh = Mesh(mesh.devices.reshape(4, 4, 2, 2, 4), (*SEQ, "head"))
    return jax.shard_map(
        local,
        mesh=mesh,
        in_specs=(
            P((*SEQ, "head"), None),
            P((*SEQ, "head"), None),
            P((*SEQ, "head"), None),
            P("head", SEQ),
            P(None, "head", None, None),
            P("head"),
            P("head", None),
        ),
        out_specs=(P((*SEQ, "head"), None), P(None, "head", None, None)),
        check_vma=False,
    )
```

```python
import math
import jax
import jax.numpy as jnp
from jax import lax
from jax.experimental import pallas as pl
from jax.experimental.pallas import tpu as pltpu
from jax.sharding import Mesh, PartitionSpec as P


NS_ITERS = 3
epsilon = 1e-06
coef_linear = 3.4445
coef_square = -4.775
coef_cubic = 2.0315


def split(value):
    high = value.astype(jnp.bfloat16)
    low = (value - high.astype(jnp.float32)).astype(jnp.bfloat16)
    return high, low


def dot3(left, right, contract):
    dims = (contract, ((), ()))
    (lh, ll), (rh, rl) = left, right
    prod = lambda a, b: lax.dot_general(a, b, dims, preferred_element_type=jnp.float32)
    return prod(lh, rh) + (prod(lh, rl) + prod(ll, rh))


NN = ((1,), (0,))
NT = ((1,), (1,))
TN = ((0,), (0,))


def rows_of(ref):
    return ref[...].reshape(-1, ref.shape[-1])


def joined(*refs):
    return jnp.concatenate([ref[...] for ref in refs], axis=0)


def gradient_kernel(k_ref, v_ref, s_ref, w_ref, g_ref):
    key = split(rows_of(k_ref))
    upstream = split(-s_ref[...] * rows_of(v_ref))
    gate_pre = dot3(key, split(w_ref[0]), NN)
    up_pre = dot3(key, split(w_ref[2]), NN)
    back = dot3(upstream, split(w_ref[1]), NN)
    sig = jax.nn.sigmoid(gate_pre)
    active = gate_pre * sig
    g_ref[1] = dot3(upstream, split(active * up_pre), TN)
    g_ref[2] = dot3(key, split(back * active), TN)
    slope = sig * (1.0 + gate_pre * (1.0 - sig))
    g_ref[0] = dot3(key, split(back * up_pre * slope), TN)


def newton_kernel(g_ref, w_ref, o_ref):
    mats = []
    for i in range(3):
        g = g_ref[i]
        mats.append(g * (1.0 / (jnp.sqrt(jnp.sum(g * g, keepdims=True)) + epsilon)))
    for _ in range(NS_ITERS):
        parts = [split(m) for m in mats]
        grams = [dot3(p, p, NT) for p in parts]
        gparts = [split(a) for a in grams]
        polys = [coef_square * a + coef_cubic * dot3(p, p, NN) for a, p in zip(grams, gparts)]
        mats = [coef_linear * m + dot3(split(b), p, NN) for m, b, p in zip(mats, polys, parts)]
    for i in range(3):
        w = w_ref[i]
        c = w - mats[i]
        target = jnp.sqrt(jnp.sum(w * w, axis=0, keepdims=True))
        current = jnp.sqrt(jnp.sum(c * c, axis=0, keepdims=True)) + epsilon
        o_ref[i] = c * (target / current)


def attention_kernel(first_ref, order_ref, qa, qb, qc, qd, kp_ref, k_ref, vp_ref, v_ref, o_ref):
    q = split(joined(qa, qb, qc, qd))
    scale = 1.0 / math.sqrt(o_ref.shape[-1])
    prev = dot3(q, split(rows_of(kp_ref)), NT) * scale
    here = dot3(q, split(rows_of(k_ref)), NT) * scale
    row = lax.broadcasted_iota(jnp.int32, prev.shape, 0)
    col = lax.broadcasted_iota(jnp.int32, prev.shape, 1)
    prev = jnp.where((col > row) & (first_ref[0] > 0), prev, -1e30)
    here = jnp.where(col <= row, here, -1e30)
    top = jnp.maximum(jnp.max(prev, axis=1, keepdims=True), jnp.max(here, axis=1, keepdims=True))
    ep, eh = jnp.exp(prev - top), jnp.exp(here - top)
    total = jnp.sum(ep, axis=1, keepdims=True) + jnp.sum(eh, axis=1, keepdims=True)
    acc = dot3(split(ep), split(rows_of(vp_ref)), NN) + dot3(split(eh), split(rows_of(v_ref)), NN)
    o_ref[...] = acc / total


def apply_head(qa, qb, qc, qd, w_ref, att_ref, gain_ref):
    q = split(joined(qa, qb, qc, qd))
    gate_pre = dot3(q, split(w_ref[0]), NN)
    up_pre = dot3(q, split(w_ref[2]), NN)
    glu = gate_pre * jax.nn.sigmoid(gate_pre) * up_pre
    fast = dot3(split(glu), split(w_ref[1]), NT)
    fast = fast * lax.rsqrt(jnp.mean(fast * fast, axis=1, keepdims=True) + epsilon)
    return fast * gain_ref[...] + att_ref[...]


def apply_first_kernel(head_ref, order_ref, *refs):
    *given, o_ref = refs
    o_ref[...] = apply_head(*given)


def apply_second_kernel(head_ref, order_ref, *refs):
    *given, done_ref, o_ref = refs
    value = apply_head(*given)
    done = done_ref[...]
    is_first = head_ref[0] == 0
    dim = value.shape[1]
    shape = (o_ref.shape[0], o_ref.shape[1], dim)
    o_ref[:, :, :dim] = jnp.where(is_first, value, done).reshape(shape)
    o_ref[:, :, dim:] = jnp.where(is_first, done, value).reshape(shape)


def slice_kernel(place_ref, w_ref, o_ref):
    o_ref[...] = w_ref[...].astype(jnp.float32)


def project_kernel(place_ref, order_ref, *refs):
    lefts, (far_ref, near_ref, mine_ref, theirs_ref) = refs[:8], refs[8:]
    total = None
    for slot in range(4):
        rows = jnp.concatenate([lefts[slot][...], lefts[4 + slot][...]], axis=0)
        right = near_ref[...] if slot == 0 else rows_of(far_ref.at[:, slot - 1]).astype(jnp.bfloat16)
        value = jnp.dot(rows.astype(jnp.bfloat16), right, preferred_element_type=jnp.float32)
        total = value if total is None else total + value
    half = total.shape[0] // 2
    mine_ref[...] = total[:half]
    theirs_ref[...] = total[half:]


def finish_kernel(place_ref, mine_ref, given_ref, o_ref):
    is_first = place_ref[0] == 0
    mine, given = mine_ref[...], given_ref[...]
    width = mine.shape[1]
    o_ref[:, :width] = jnp.where(is_first, mine, given).astype(o_ref.dtype)
    o_ref[:, width:] = jnp.where(is_first, given, mine).astype(o_ref.dtype)


def assemble_kernel(place_ref, mine_ref, given_ref, o_ref):
    is_first = place_ref[0] == 0
    mine, given = mine_ref[...], given_ref[...]
    o_ref[:, 0] = jnp.where(is_first, mine, given)
    o_ref[:, 1] = jnp.where(is_first, given, mine)


SEQ = ("x", "y", "zh", "core")
HEAD_DIM = 256
PARAMS = pltpu.CompilerParams(vmem_limit_bytes=24 * 2**20)


def head_gradient(pairs, steps, weights, head):
    dim, hidden = weights.shape[2:]
    length = steps.shape[1]
    ranks, _, rows, _ = pairs.shape
    spec = pltpu.PrefetchScalarGridSpec(
        num_scalar_prefetch=1,
        grid=(1,),
        in_specs=[
            pl.BlockSpec((ranks, None, rows, dim), lambda i, h: (0, 0, 0, h[0])),
            pl.BlockSpec((ranks, None, rows, dim), lambda i, h: (0, 1, 0, h[0])),
            pl.BlockSpec((None, length, 1), lambda i, h: (h[0], 0, 0)),
            pl.BlockSpec((3, None, dim, hidden), lambda i, h: (0, h[0], 0, 0)),
        ],
        out_specs=pl.BlockSpec((3, dim, hidden), lambda i, h: (0, 0, 0)),
    )
    return pl.pallas_call(
        lambda h, *refs: gradient_kernel(*refs),
        grid_spec=spec,
        out_shape=jax.ShapeDtypeStruct((3, dim, hidden), jnp.float32),
        compiler_params=PARAMS,
        name="gradient",
    )(head, pairs, pairs, steps, in_hbm(weights))


def newton(grads, weights, head):
    _, dim, hidden = grads.shape
    spec = pltpu.PrefetchScalarGridSpec(
        num_scalar_prefetch=1,
        grid=(1,),
        in_specs=[
            pl.BlockSpec((3, dim, hidden), lambda i, h: (0, 0, 0)),
            pl.BlockSpec((3, None, dim, hidden), lambda i, h: (0, h[0], 0, 0)),
        ],
        out_specs=pl.BlockSpec((3, dim, hidden), lambda i, h: (0, 0, 0)),
    )
    return pl.pallas_call(
        lambda h, *refs: newton_kernel(*refs),
        grid_spec=spec,
        out_shape=jax.ShapeDtypeStruct((3, dim, hidden), jnp.float32),
        compiler_params=PARAMS,
        name="newton",
    )(head, in_hbm(grads), in_hbm(weights))


def query_specs(rows, dim, column):
    def block(source):
        return pl.BlockSpec(
            (None, rows, dim), lambda i, f, order: (order[source], 0, column(i, f))
        )

    return [block(source) for source in range(4)]


def attention(first, order, queries, before, pairs):
    ranks, _, rows, width = pairs.shape
    dim = HEAD_DIM
    length = ranks * rows
    key = pl.BlockSpec((ranks, None, rows, dim), lambda i, f, order: (0, 0, 0, i))
    value = pl.BlockSpec((ranks, None, rows, dim), lambda i, f, order: (0, 1, 0, i))
    return pl.pallas_call(
        attention_kernel,
        grid_spec=pltpu.PrefetchScalarGridSpec(
            num_scalar_prefetch=2,
            grid=(width // dim,),
            in_specs=[*query_specs(rows, dim, lambda i, f: i), key, key, value, value],
            out_specs=pl.BlockSpec((length, dim), lambda i, f, order: (0, i)),
        ),
        out_shape=jax.ShapeDtypeStruct((length, width), jnp.float32),
        compiler_params=PARAMS,
        name="attention",
    )(first, order, *[queries] * 4, before, pairs, before, pairs)


def apply_fast(head, order, queries, weights, attended, gain, done=None):
    ranks, rows, width = queries.shape
    length = ranks * rows
    _, dim, hidden = weights.shape
    specs = [
        *query_specs(rows, dim, lambda i, h: h[0]),
        pl.BlockSpec((3, dim, hidden), lambda i, h, order: (0, 0, 0)),
        pl.BlockSpec((length, dim), lambda i, h, order: (0, h[0])),
        pl.BlockSpec((1, dim), lambda i, h, order: (0, h[0])),
    ]
    if done is not None:
        specs.append(pl.BlockSpec((length, dim), lambda i, h, order: (0, 0)))
    if done is None:
        out_shape = (length, dim)
    else:
        out_shape = (ranks, rows, width)
    return pl.pallas_call(
        apply_first_kernel if done is None else apply_second_kernel,
        grid_spec=pltpu.PrefetchScalarGridSpec(
            num_scalar_prefetch=2,
            grid=(1,),
            in_specs=specs,
            out_specs=pl.BlockSpec(out_shape, lambda i, h, order: (0,) * len(out_shape)),
        ),
        out_shape=jax.ShapeDtypeStruct(out_shape, jnp.float32),
        compiler_params=PARAMS,
    )(head, order, *[queries] * 4, weights, attended, gain, *(() if done is None else (done,)))


def weight_slice(w_out, part, core):
    rows, width = w_out.shape[0] // 16, w_out.shape[1] // 2
    place = jnp.stack([part, core])
    return pl.pallas_call(
        slice_kernel,
        grid_spec=pltpu.PrefetchScalarGridSpec(
            num_scalar_prefetch=1,
            grid=(1,),
            in_specs=[pl.BlockSpec((rows, width), lambda i, p: (p[0], p[1]))],
            out_specs=pl.BlockSpec((rows, width), lambda i, p: (0, 0)),
        ),
        out_shape=jax.ShapeDtypeStruct((rows, width), jnp.float32),
        compiler_params=PARAMS,
        name="weight_slice",
    )(place, in_hbm(w_out))


def project(core, order, mine, theirs, far, near):
    _, rows, dim = mine.shape
    parts, others, piece, width = far.shape
    block = width // 4

    def left(slot):
        return pl.BlockSpec((None, rows, dim), lambda i, c, order: (order[slot], 0, 0))

    out = pl.BlockSpec((rows, block), lambda i, c, order: (0, i))
    return pl.pallas_call(
        project_kernel,
        grid_spec=pltpu.PrefetchScalarGridSpec(
            num_scalar_prefetch=2,
            grid=(width // block,),
            in_specs=[
                *[left(slot) for slot in range(4)] * 2,
                pl.BlockSpec((parts, others, piece, block), lambda i, c, order: (0, 0, 0, i)),
                pl.BlockSpec((dim, block), lambda i, c, order: (0, c[0] * (width // block) + i)),
            ],
            out_specs=[out, out],
        ),
        out_shape=[jax.ShapeDtypeStruct((rows, width), jnp.float32)] * 2,
        compiler_params=pltpu.CompilerParams(vmem_limit_bytes=40 * 2**20),
        name="project",
    )(core, order, *[mine] * 4, *[theirs] * 4, in_hbm(far), in_hbm(near))


def finish(core, mine, given):
    rows, width = mine.shape
    block = pl.BlockSpec((rows, width), lambda i, c: (0, 0))
    return pl.pallas_call(
        finish_kernel,
        grid_spec=pltpu.PrefetchScalarGridSpec(
            num_scalar_prefetch=1,
            grid=(1,),
            in_specs=[block, block],
            out_specs=pl.BlockSpec((rows, 2 * width), lambda i, c: (0, 0)),
        ),
        out_shape=jax.ShapeDtypeStruct((rows, 2 * width), jnp.bfloat16),
        compiler_params=PARAMS,
        name="finish",
    )(core, mine, given)


def assemble(core, mine, given):
    kinds, dim, hidden = mine.shape
    block = pl.BlockSpec((1, dim, hidden), lambda i, c: (i, 0, 0))
    return pl.pallas_call(
        assemble_kernel,
        grid_spec=pltpu.PrefetchScalarGridSpec(
            num_scalar_prefetch=1,
            grid=(kinds,),
            in_specs=[block, block],
            out_specs=pl.BlockSpec((1, 2, dim, hidden), lambda i, c: (i, 0, 0, 0)),
        ),
        out_shape=jax.ShapeDtypeStruct((kinds, 2, dim, hidden), jnp.float32),
        compiler_params=PARAMS,
        name="assemble",
    )(core, mine, given)


def by_head(rows):
    length, width = rows.shape
    return rows.reshape(length, 4, width // 4).transpose(1, 0, 2)


def exchange(value, axes):
    return lax.all_to_all(value, axes, split_axis=0, concat_axis=0, tiled=True)


def turned(value, step):
    return lax.ppermute(value, "head", [(rank, (rank + step) % 4) for rank in range(4)])


def rotated_heads(rows):
    width = rows.shape[1] // 4
    here = lax.axis_index("head")
    parts = []
    for step in range(4):
        column = lax.rem(here + step, 4) * width
        part = lax.dynamic_slice_in_dim(rows, column, width, axis=1)
        parts.append(turned(part, step) if step else part)
    order = jnp.stack([lax.rem(here + 4 - source, 4) for source in range(4)])
    return jnp.stack(parts), order


def in_hbm(value):
    return pltpu.with_memory_space_constraint(value, pltpu.HBM)


def swap_cores(value):
    return lax.ppermute(value, "core", [(0, 1), (1, 0)])


def sum_rest(value):
    shape = value.shape
    pieces = exchange(value.reshape(16, -1, shape[-1]), ("x", "y"))
    part = jnp.sum(pieces, axis=0)
    part = part + lax.ppermute(part, "zh", [(0, 1), (1, 0)])
    return exchange(jnp.broadcast_to(part, (16, *part.shape)), ("x", "y")).reshape(shape)


def earlier(value):
    return lax.ppermute(value, SEQ, [(source, source + 1) for source in range(63)])


def local(q_rows, k_rows, v_rows, step_sizes, fast_weights, norm_gain, w_out):
    core, here = lax.axis_index("core"), lax.axis_index("head")
    mine, other = core.reshape(1), (1 - core).reshape(1)
    first = lax.axis_index(SEQ).reshape(1)
    steps = step_sizes[:, :, None]
    gain = norm_gain.reshape(1, -1)
    pairs = exchange(jnp.stack([by_head(k_rows), by_head(v_rows)], axis=1), "head")
    part = weight_slice(w_out, lax.axis_index("x") * 4 + lax.axis_index("y"), core)
    far_part = jnp.stack([turned(part, step) for step in (1, 2, 3)])
    far_weights = lax.all_gather(far_part, ("x", "y"))
    given = head_gradient(pairs, steps, fast_weights, other)
    received = swap_cores(given)
    kept = head_gradient(pairs, steps, fast_weights, mine)
    before = earlier(pairs)
    total = sum_rest(kept + received)
    updated = newton(total, fast_weights, mine)
    partner = swap_cores(updated)
    queries, order = rotated_heads(q_rows)
    attended = attention(first, order, queries, before, pairs)
    done = apply_fast(mine, order, queries, updated, attended, gain)
    combined = apply_fast(other, order, queries, partner, attended, gain, done)
    own_rows = exchange(combined, "head")
    their_rows = swap_cores(own_rows)
    turn = jnp.stack([lax.rem(here + 4 - step, 4) for step in range(4)])
    kept_out, given_out = project(mine, turn, own_rows, their_rows, far_weights, w_out)
    other_half = swap_cores(given_out)
    mixed = finish(mine, kept_out, other_half)
    new_weights = assemble(mine, in_hbm(updated), in_hbm(partner))
    return (mixed, new_weights)


def solution(mesh):
    mesh = Mesh(mesh.devices.reshape(4, 4, 2, 2, 4), (*SEQ, "head"))
    return jax.shard_map(
        local,
        mesh=mesh,
        in_specs=(
            P((*SEQ, "head"), None),
            P((*SEQ, "head"), None),
            P((*SEQ, "head"), None),
            P("head", SEQ),
            P(None, "head", None, None),
            P("head"),
            P("head", None),
        ),
        out_specs=(P((*SEQ, "head"), None), P(None, "head", None, None)),
        check_vma=False,
    )
```

```python
import math
import jax
import jax.numpy as jnp
from jax import lax
from jax.experimental import pallas as pl
from jax.experimental.pallas import tpu as pltpu
from jax.sharding import Mesh, PartitionSpec as P


NS_ITERS = 3
epsilon = 1e-06
coef_linear = 3.4445
coef_square = -4.775
coef_cubic = 2.0315


def split(value):
    high = value.astype(jnp.bfloat16)
    low = (value - high.astype(jnp.float32)).astype(jnp.bfloat16)
    return high, low


def dot3(left, right, contract):
    dims = (contract, ((), ()))
    (lh, ll), (rh, rl) = left, right
    prod = lambda a, b: lax.dot_general(a, b, dims, preferred_element_type=jnp.float32)
    return prod(lh, rh) + (prod(lh, rl) + prod(ll, rh))


NN = ((1,), (0,))
NT = ((1,), (1,))
TN = ((0,), (0,))


def rows_of(ref):
    return ref[...].reshape(-1, ref.shape[-1])


def joined(*refs):
    return jnp.concatenate([ref[...] for ref in refs], axis=0)


def gradient_kernel(k_ref, v_ref, s_ref, w_ref, g_ref):
    key = split(rows_of(k_ref))
    upstream = split(-s_ref[...] * rows_of(v_ref))
    gate_pre = dot3(key, split(w_ref[0]), NN)
    up_pre = dot3(key, split(w_ref[2]), NN)
    back = dot3(upstream, split(w_ref[1]), NN)
    sig = jax.nn.sigmoid(gate_pre)
    active = gate_pre * sig
    g_ref[1] = dot3(upstream, split(active * up_pre), TN)
    g_ref[2] = dot3(key, split(back * active), TN)
    slope = sig * (1.0 + gate_pre * (1.0 - sig))
    g_ref[0] = dot3(key, split(back * up_pre * slope), TN)


def newton_kernel(g_ref, w_ref, o_ref):
    mats = []
    for i in range(3):
        g = g_ref[i]
        mats.append(g * (1.0 / (jnp.sqrt(jnp.sum(g * g, keepdims=True)) + epsilon)))
    for _ in range(NS_ITERS):
        parts = [split(m) for m in mats]
        grams = [dot3(p, p, NT) for p in parts]
        gparts = [split(a) for a in grams]
        polys = [coef_square * a + coef_cubic * dot3(p, p, NN) for a, p in zip(grams, gparts)]
        mats = [coef_linear * m + dot3(split(b), p, NN) for m, b, p in zip(mats, polys, parts)]
    for i in range(3):
        w = w_ref[i]
        c = w - mats[i]
        target = jnp.sqrt(jnp.sum(w * w, axis=0, keepdims=True))
        current = jnp.sqrt(jnp.sum(c * c, axis=0, keepdims=True)) + epsilon
        o_ref[i] = c * (target / current)


def attention_kernel(first_ref, order_ref, qa, qb, qc, qd, kp_ref, k_ref, vp_ref, v_ref, o_ref):
    q = split(joined(qa, qb, qc, qd))
    scale = 1.0 / math.sqrt(o_ref.shape[-1])
    prev = dot3(q, split(rows_of(kp_ref)), NT) * scale
    here = dot3(q, split(rows_of(k_ref)), NT) * scale
    row = lax.broadcasted_iota(jnp.int32, prev.shape, 0)
    col = lax.broadcasted_iota(jnp.int32, prev.shape, 1)
    prev = jnp.where((col > row) & (first_ref[0] > 0), prev, -1e30)
    here = jnp.where(col <= row, here, -1e30)
    top = jnp.maximum(jnp.max(prev, axis=1, keepdims=True), jnp.max(here, axis=1, keepdims=True))
    ep, eh = jnp.exp(prev - top), jnp.exp(here - top)
    total = jnp.sum(ep, axis=1, keepdims=True) + jnp.sum(eh, axis=1, keepdims=True)
    acc = dot3(split(ep), split(rows_of(vp_ref)), NN) + dot3(split(eh), split(rows_of(v_ref)), NN)
    o_ref[...] = acc / total


def apply_head(qa, qb, qc, qd, w_ref, att_ref, gain_ref):
    q = split(joined(qa, qb, qc, qd))
    gate_pre = dot3(q, split(w_ref[0]), NN)
    up_pre = dot3(q, split(w_ref[2]), NN)
    glu = gate_pre * jax.nn.sigmoid(gate_pre) * up_pre
    fast = dot3(split(glu), split(w_ref[1]), NT)
    fast = fast * lax.rsqrt(jnp.mean(fast * fast, axis=1, keepdims=True) + epsilon)
    return fast * gain_ref[...] + att_ref[...]


def apply_first_kernel(head_ref, order_ref, *refs):
    *given, o_ref = refs
    o_ref[...] = apply_head(*given)


def apply_second_kernel(head_ref, order_ref, *refs):
    *given, done_ref, o_ref = refs
    value = apply_head(*given)
    done = done_ref[...]
    is_first = head_ref[0] == 0
    dim = value.shape[1]
    shape = (o_ref.shape[0], o_ref.shape[1], dim)
    o_ref[:, :, :dim] = jnp.where(is_first, value, done).reshape(shape)
    o_ref[:, :, dim:] = jnp.where(is_first, done, value).reshape(shape)


def slice_kernel(place_ref, w_ref, o_ref):
    o_ref[...] = w_ref[...].astype(jnp.float32)


def project_kernel(place_ref, order_ref, *refs):
    lefts, (far_ref, edge_ref, near_ref, mine_ref, theirs_ref) = refs[:8], refs[8:]
    edge = edge_ref.shape[1]
    piece = (far_ref.shape[1] + edge) // 3
    total = None
    for slot in range(4):
        rows = jnp.concatenate([lefts[slot][...], lefts[4 + slot][...]], axis=0)
        if slot == 0:
            right = near_ref[...]
        elif slot == 3:
            parts = [far_ref[:, 2 * piece :], edge_ref[...]]
            right = jnp.concatenate(parts, axis=1).reshape(near_ref.shape).astype(jnp.bfloat16)
        else:
            parts = far_ref[:, (slot - 1) * piece : slot * piece]
            right = parts.reshape(near_ref.shape).astype(jnp.bfloat16)
        value = jnp.dot(rows.astype(jnp.bfloat16), right, preferred_element_type=jnp.float32)
        total = value if total is None else total + value
    half = total.shape[0] // 2
    mine_ref[...] = total[:half]
    theirs_ref[...] = total[half:]


def finish_kernel(place_ref, mine_ref, given_ref, o_ref):
    is_first = place_ref[0] == 0
    mine, given = mine_ref[...], given_ref[...]
    width = mine.shape[1]
    o_ref[:, :width] = jnp.where(is_first, mine, given).astype(o_ref.dtype)
    o_ref[:, width:] = jnp.where(is_first, given, mine).astype(o_ref.dtype)


def assemble_kernel(place_ref, mine_ref, given_ref, o_ref):
    is_first = place_ref[0] == 0
    mine, given = mine_ref[...], given_ref[...]
    o_ref[:, 0] = jnp.where(is_first, mine, given)
    o_ref[:, 1] = jnp.where(is_first, given, mine)


SEQ = ("x", "y", "zh", "core")
HEAD_DIM = 256
EDGE = 8
PARAMS = pltpu.CompilerParams(vmem_limit_bytes=24 * 2**20)


def head_gradient(pairs, steps, weights, head):
    dim, hidden = weights.shape[2:]
    length = steps.shape[1]
    ranks, _, rows, _ = pairs.shape
    spec = pltpu.PrefetchScalarGridSpec(
        num_scalar_prefetch=1,
        grid=(1,),
        in_specs=[
            pl.BlockSpec((ranks, None, rows, dim), lambda i, h: (0, 0, 0, h[0])),
            pl.BlockSpec((ranks, None, rows, dim), lambda i, h: (0, 1, 0, h[0])),
            pl.BlockSpec((None, length, 1), lambda i, h: (h[0], 0, 0)),
            pl.BlockSpec((3, None, dim, hidden), lambda i, h: (0, h[0], 0, 0)),
        ],
        out_specs=pl.BlockSpec((3, dim, hidden), lambda i, h: (0, 0, 0)),
    )
    return pl.pallas_call(
        lambda h, *refs: gradient_kernel(*refs),
        grid_spec=spec,
        out_shape=jax.ShapeDtypeStruct((3, dim, hidden), jnp.float32),
        compiler_params=PARAMS,
        name="gradient",
    )(head, pairs, pairs, steps, in_hbm(weights))


def newton(grads, weights, head):
    _, dim, hidden = grads.shape
    spec = pltpu.PrefetchScalarGridSpec(
        num_scalar_prefetch=1,
        grid=(1,),
        in_specs=[
            pl.BlockSpec((3, dim, hidden), lambda i, h: (0, 0, 0)),
            pl.BlockSpec((3, None, dim, hidden), lambda i, h: (0, h[0], 0, 0)),
        ],
        out_specs=pl.BlockSpec((3, dim, hidden), lambda i, h: (0, 0, 0)),
    )
    return pl.pallas_call(
        lambda h, *refs: newton_kernel(*refs),
        grid_spec=spec,
        out_shape=jax.ShapeDtypeStruct((3, dim, hidden), jnp.float32),
        compiler_params=PARAMS,
        name="newton",
    )(head, in_hbm(grads), in_hbm(weights))


def query_specs(rows, dim, column):
    def block(source):
        return pl.BlockSpec(
            (None, rows, dim), lambda i, f, order: (order[source], 0, column(i, f))
        )

    return [block(source) for source in range(4)]


def attention(first, order, queries, before, pairs):
    ranks, _, rows, width = pairs.shape
    dim = HEAD_DIM
    length = ranks * rows
    key = pl.BlockSpec((ranks, None, rows, dim), lambda i, f, order: (0, 0, 0, i))
    value = pl.BlockSpec((ranks, None, rows, dim), lambda i, f, order: (0, 1, 0, i))
    return pl.pallas_call(
        attention_kernel,
        grid_spec=pltpu.PrefetchScalarGridSpec(
            num_scalar_prefetch=2,
            grid=(width // dim,),
            in_specs=[*query_specs(rows, dim, lambda i, f: i), key, key, value, value],
            out_specs=pl.BlockSpec((length, dim), lambda i, f, order: (0, i)),
        ),
        out_shape=jax.ShapeDtypeStruct((length, width), jnp.float32),
        compiler_params=PARAMS,
        name="attention",
    )(first, order, *[queries] * 4, in_hbm(before), pairs, in_hbm(before), pairs)


def apply_fast(head, order, queries, weights, attended, gain, done=None):
    ranks, rows, width = queries.shape
    length = ranks * rows
    _, dim, hidden = weights.shape
    specs = [
        *query_specs(rows, dim, lambda i, h: h[0]),
        pl.BlockSpec((3, dim, hidden), lambda i, h, order: (0, 0, 0)),
        pl.BlockSpec((length, dim), lambda i, h, order: (0, h[0])),
        pl.BlockSpec((1, dim), lambda i, h, order: (0, h[0])),
    ]
    if done is not None:
        specs.append(pl.BlockSpec((length, dim), lambda i, h, order: (0, 0)))
    if done is None:
        out_shape = (length, dim)
    else:
        out_shape = (ranks, rows, width)
    return pl.pallas_call(
        apply_first_kernel if done is None else apply_second_kernel,
        grid_spec=pltpu.PrefetchScalarGridSpec(
            num_scalar_prefetch=2,
            grid=(1,),
            in_specs=specs,
            out_specs=pl.BlockSpec(out_shape, lambda i, h, order: (0,) * len(out_shape)),
        ),
        out_shape=jax.ShapeDtypeStruct(out_shape, jnp.float32),
        compiler_params=PARAMS,
    )(head, order, *[queries] * 4, weights, attended, gain, *(() if done is None else (done,)))


def weight_slice(w_out, part, core):
    rows, width = w_out.shape[0] // 16, w_out.shape[1] // 2
    place = jnp.stack([part, core])
    return pl.pallas_call(
        slice_kernel,
        grid_spec=pltpu.PrefetchScalarGridSpec(
            num_scalar_prefetch=1,
            grid=(1,),
            in_specs=[pl.BlockSpec((rows, width), lambda i, p: (p[0], p[1]))],
            out_specs=pl.BlockSpec((rows, width), lambda i, p: (0, 0)),
        ),
        out_shape=jax.ShapeDtypeStruct((rows, width), jnp.float32),
        compiler_params=PARAMS,
        name="weight_slice",
    )(place, in_hbm(w_out))


def weight_edge(w_out, core):
    rows, width = w_out.shape[0] // 16, w_out.shape[1] // 2
    return pl.pallas_call(
        slice_kernel,
        grid_spec=pltpu.PrefetchScalarGridSpec(
            num_scalar_prefetch=1,
            grid=(1,),
            in_specs=[
                pl.BlockSpec((16, EDGE, width), lambda i, c: (0, rows // EDGE - 1, c[0]))
            ],
            out_specs=pl.BlockSpec((16, EDGE, width), lambda i, c: (0, 0, 0)),
        ),
        out_shape=jax.ShapeDtypeStruct((16, EDGE, width), jnp.float32),
        compiler_params=PARAMS,
        name="weight_edge",
    )(core, in_hbm(w_out.reshape(16, rows, w_out.shape[1])))


def project(core, order, mine, theirs, far, edge, near):
    _, rows, dim = mine.shape
    parts, kept, width = far.shape
    block = width // 4

    def left(slot):
        return pl.BlockSpec((None, rows, dim), lambda i, c, order: (order[slot], 0, 0))

    out = pl.BlockSpec((rows, block), lambda i, c, order: (0, i))
    return pl.pallas_call(
        project_kernel,
        grid_spec=pltpu.PrefetchScalarGridSpec(
            num_scalar_prefetch=2,
            grid=(width // block,),
            in_specs=[
                *[left(slot) for slot in range(4)] * 2,
                pl.BlockSpec((parts, kept, block), lambda i, c, order: (0, 0, i)),
                pl.BlockSpec((parts, edge.shape[1], block), lambda i, c, order: (0, 0, i)),
                pl.BlockSpec((dim, block), lambda i, c, order: (0, c[0] * (width // block) + i)),
            ],
            out_specs=[out, out],
        ),
        out_shape=[jax.ShapeDtypeStruct((rows, width), jnp.float32)] * 2,
        compiler_params=pltpu.CompilerParams(vmem_limit_bytes=40 * 2**20),
        name="project",
    )(core, order, *[mine] * 4, *[theirs] * 4, in_hbm(far), in_hbm(edge), in_hbm(near))


def finish(core, mine, given):
    rows, width = mine.shape
    block = pl.BlockSpec((rows, width), lambda i, c: (0, 0))
    return pl.pallas_call(
        finish_kernel,
        grid_spec=pltpu.PrefetchScalarGridSpec(
            num_scalar_prefetch=1,
            grid=(1,),
            in_specs=[block, block],
            out_specs=pl.BlockSpec((rows, 2 * width), lambda i, c: (0, 0)),
        ),
        out_shape=jax.ShapeDtypeStruct((rows, 2 * width), jnp.bfloat16),
        compiler_params=PARAMS,
        name="finish",
    )(core, mine, given)


def assemble(core, mine, given):
    kinds, dim, hidden = mine.shape
    block = pl.BlockSpec((1, dim, hidden), lambda i, c: (i, 0, 0))
    return pl.pallas_call(
        assemble_kernel,
        grid_spec=pltpu.PrefetchScalarGridSpec(
            num_scalar_prefetch=1,
            grid=(kinds,),
            in_specs=[block, block],
            out_specs=pl.BlockSpec((1, 2, dim, hidden), lambda i, c: (i, 0, 0, 0)),
        ),
        out_shape=jax.ShapeDtypeStruct((kinds, 2, dim, hidden), jnp.float32),
        compiler_params=PARAMS,
        name="assemble",
    )(core, mine, given)


def by_head(rows):
    length, width = rows.shape
    return rows.reshape(length, 4, width // 4).transpose(1, 0, 2)


def exchange(value, axes):
    return lax.all_to_all(value, axes, split_axis=0, concat_axis=0, tiled=True)


def turned(value, step):
    return lax.ppermute(value, "head", [(rank, (rank + step) % 4) for rank in range(4)])


def rotated_heads(rows):
    width = rows.shape[1] // 4
    here = lax.axis_index("head")
    parts = []
    for step in range(4):
        column = lax.rem(here + step, 4) * width
        part = lax.dynamic_slice_in_dim(rows, column, width, axis=1)
        parts.append(turned(part, step) if step else part)
    order = jnp.stack([lax.rem(here + 4 - source, 4) for source in range(4)])
    return jnp.stack(parts), order


def in_hbm(value):
    return pltpu.with_memory_space_constraint(value, pltpu.HBM)


def swap_cores(value):
    return lax.ppermute(value, "core", [(0, 1), (1, 0)])


def sum_rest(value):
    shape = value.shape
    pieces = exchange(value.reshape(16, -1, shape[-1]), ("x", "y"))
    part = jnp.sum(pieces, axis=0)
    part = part + lax.ppermute(part, "zh", [(0, 1), (1, 0)])
    return exchange(jnp.broadcast_to(part, (16, *part.shape)), ("x", "y")).reshape(shape)


def earlier(value):
    return lax.ppermute(value, SEQ, [(source, source + 1) for source in range(63)])


def local(q_rows, k_rows, v_rows, step_sizes, fast_weights, norm_gain, w_out):
    core, here = lax.axis_index("core"), lax.axis_index("head")
    mine, other = core.reshape(1), (1 - core).reshape(1)
    first = lax.axis_index(SEQ).reshape(1)
    steps = step_sizes[:, :, None]
    gain = norm_gain.reshape(1, -1)
    pairs = exchange(jnp.stack([by_head(k_rows), by_head(v_rows)], axis=1), "head")
    part = weight_slice(w_out, lax.axis_index("x") * 4 + lax.axis_index("y"), core)
    steps_part = (part, part, part[:-EDGE])
    far_part = jnp.concatenate([turned(value, step) for step, value in enumerate(steps_part, 1)])
    far_weights = lax.all_gather(far_part, ("x", "y"))
    edge_part = weight_edge(w_out, mine)
    edge = turned(edge_part, 3)
    given = head_gradient(pairs, steps, fast_weights, other)
    received = swap_cores(given)
    kept = head_gradient(pairs, steps, fast_weights, mine)
    before = earlier(pairs)
    total = sum_rest(kept + received)
    updated = newton(total, fast_weights, mine)
    partner = swap_cores(updated)
    queries, order = rotated_heads(q_rows)
    attended = attention(first, order, queries, before, pairs)
    done = apply_fast(mine, order, queries, updated, attended, gain)
    combined = apply_fast(other, order, queries, partner, attended, gain, done)
    own_rows = exchange(combined, "head")
    their_rows = swap_cores(own_rows)
    turn = jnp.stack([lax.rem(here + 4 - step, 4) for step in range(4)])
    kept_out, given_out = project(mine, turn, own_rows, their_rows, far_weights, edge, w_out)
    other_half = swap_cores(given_out)
    mixed = finish(mine, kept_out, other_half)
    new_weights = assemble(mine, in_hbm(updated), in_hbm(partner))
    return (mixed, new_weights)


def solution(mesh):
    mesh = Mesh(mesh.devices.reshape(4, 4, 2, 2, 4), (*SEQ, "head"))
    return jax.shard_map(
        local,
        mesh=mesh,
        in_specs=(
            P((*SEQ, "head"), None),
            P((*SEQ, "head"), None),
            P((*SEQ, "head"), None),
            P("head", SEQ),
            P(None, "head", None, None),
            P("head"),
            P("head", None),
        ),
        out_specs=(P((*SEQ, "head"), None), P(None, "head", None, None)),
        check_vma=False,
    )
```
